32 devices in a mesh: head: 2 (over y), ctx: 16 (over z, x, core).
Axes of the slice: x: 2, y: 2, z: 4, core: 2. Of those that a mesh axis runs over, the one named last changes fastest.
Arguments:
- queries: bfloat16 [512, 24576], P(None, 'head'), may hold values from -100 to 100
- attn_keys: bfloat16 [4096, 24576], P('ctx', 'head'), may hold values from -6 to 6
- index_queries: bfloat16 [512, 8192], P(None, 'head'), may hold values from -16 to 16
- index_keys: bfloat16 [4096, 128], P('ctx'), may hold values from -6 to 6
- head_weights: float32 [512, 64], P(None, 'head'), may hold values from 0.1 to 1
- query_pos: int32 [512], replicated, may hold values from 16 to 32767
- key_offset: int32 [4096], P('ctx'), may hold values from 0 to 7
Outputs:
- index_query_grad: float32 [512, 8192], P('ctx', 'head')
- index_key_grad: float32 [4096, 128], P('ctx')
The draws below stay inside these ranges and needn't reach their ends.
All inputs are finite; a program needn't handle non-finite values.
Results may differ from the reference program's by a relative error of at most 0.0027.
Values sent between devices are 32-bit elements; how exact they have to be, the bound alone decides.
A program may use at most 128 MiB of HBM per device.

```python
import math
import jax
import jax.numpy as jnp
from jax import lax

HEADS = 128
HEAD_DIM = 192
IHEADS = 64
IDIM = 128
QUERIES = 512
STRIDE = 8
KEYS = 4096


def attn_keys_base(key):
    sub_key = jax.random.fold_in(key, 101)
    base = jnp.clip(jax.random.normal(sub_key, (KEYS, HEADS * HEAD_DIM), jnp.float32), -6.0, 6.0)
    return base


def index_keys_base(key):
    sub_key = jax.random.fold_in(key, 103)
    base = jnp.clip(jax.random.normal(sub_key, (KEYS, IDIM), jnp.float32), -6.0, 6.0)
    return base


def draw_attn_keys(key, part):
    return attn_keys_base(key).astype(jnp.bfloat16)


def draw_index_keys(key, part):
    return index_keys_base(key).astype(jnp.bfloat16)


def draw_queries(key, part):
    sub_key = jax.random.fold_in(key, 102)
    base = jnp.clip(jax.random.normal(sub_key, (QUERIES, HEADS * HEAD_DIM), jnp.float32), -6.0, 6.0)
    return base.astype(jnp.bfloat16)


def draw_index_queries(key, part):
    sub_key = jax.random.fold_in(key, 104)
    base = jnp.clip(jax.random.normal(sub_key, (QUERIES, IHEADS * IDIM), jnp.float32), -6.0, 6.0)
    return base.astype(jnp.bfloat16)


def place_ends(array, key, smallest, high):
    extent = array.shape
    spot = [jax.random.randint(jax.random.fold_in(key, axis), (), 0, extent[axis]) for axis in range(len(extent))]
    array = array.at[tuple(spot)].set(smallest)
    longest = extent.index(max(extent))
    spot[longest] = (spot[longest] + 1) % extent[longest]
    return array.at[tuple(spot)].set(high)


def block_scale(rng, extent, split, smallest, high):
    level = 1.0
    for axis_at, blocks in split:
        draws = jax.random.uniform(jax.random.fold_in(jax.random.fold_in(rng, 6), axis_at), (blocks,), jnp.float32, smallest / len(split), high / len(split))
        level = level * jnp.repeat(jnp.exp(draws), extent[axis_at] // blocks).reshape((-1,) + (1,) * (len(extent) - 1 - axis_at))
    return level


def setup_inputs(seed: int = 0) -> dict:
    streams_of = jax.random.split(jax.random.key(seed), 8)
    return {
        "queries": draw_queries(jax.random.fold_in(streams_of[7], 71), 0),
        "attn_keys": draw_attn_keys(jax.random.fold_in(streams_of[7], 71), 0),
        "index_queries": draw_index_queries(jax.random.fold_in(streams_of[7], 71), 0),
        "index_keys": draw_index_keys(jax.random.fold_in(streams_of[7], 71), 0),
        "head_weights": jnp.clip(jnp.exp(math.log(1.0) - 2.3025851 * jax.random.uniform(streams_of[4], (QUERIES, IHEADS), jnp.float32) ** block_scale(streams_of[4], (QUERIES, IHEADS), ((1, 2),), -0.2, 0.2)), 0.1, 1.0),
        "query_pos": place_ends(jax.random.randint(streams_of[5], (QUERIES,), 2 * STRIDE, STRIDE * KEYS), jax.random.fold_in(streams_of[5], 1), 2 * STRIDE, (STRIDE * KEYS) - 1).astype(jnp.int32),
        "key_offset": place_ends(jax.random.randint(streams_of[6], (KEYS,), 0, STRIDE), jax.random.fold_in(streams_of[6], 1), 0, STRIDE - 1).astype(jnp.int32),
    }


NEG_FILL = -1e+30

def reference(queries, attn_keys, index_queries, index_keys, head_weights, query_pos, key_offset):
    key_pos = STRIDE * jnp.arange(KEYS, dtype=jnp.int32) + key_offset
    visible = key_pos[None, :] <= query_pos[:, None]
    attn_scale = 1.0 / math.sqrt(HEAD_DIM)
    inv_scale = 1.0 / math.sqrt(IDIM)

    def attn_head(total, head_index):
        start = (head_index * HEAD_DIM).astype(jnp.int32)
        query_head = lax.dynamic_slice_in_dim(queries, start, HEAD_DIM, 1)
        key_head = lax.dynamic_slice_in_dim(attn_keys, start, HEAD_DIM, 1)
        scores = jnp.dot(query_head, key_head.T, preferred_element_type=jnp.float32) * attn_scale
        masked = jnp.where(visible, scores, NEG_FILL)
        top_value = lax.optimization_barrier(jnp.max(masked, axis=1, keepdims=True))
        exp_terms = jnp.where(visible, jnp.exp(masked - top_value), 0.0)
        return (total + exp_terms / lax.optimization_barrier(jnp.sum(exp_terms, axis=1, keepdims=True)), None)
    total, _ = lax.scan(attn_head, jnp.zeros((QUERIES, KEYS), jnp.float32), jnp.arange(HEADS, dtype=jnp.int32))
    target = total / HEADS

    def index_slices(head_index):
        start = (head_index * IDIM).astype(jnp.int32)
        query_head = lax.dynamic_slice_in_dim(index_queries, start, IDIM, 1)
        activation = jnp.dot(query_head, index_keys.T, preferred_element_type=jnp.float32) * inv_scale
        weight_col = lax.dynamic_slice_in_dim(head_weights, head_index.astype(jnp.int32), 1, 1)
        return (query_head, activation, weight_col)

    def index_head(logits, head_index):
        query_head, activation, weight_col = index_slices(head_index)
        return (logits + weight_col * jnp.maximum(activation, 0.0), None)
    logits, _ = lax.scan(index_head, jnp.zeros((QUERIES, KEYS), jnp.float32), jnp.arange(IHEADS, dtype=jnp.int32))
    masked = jnp.where(visible, logits, NEG_FILL)
    top_value = lax.optimization_barrier(jnp.max(masked, axis=1, keepdims=True))
    exp_terms = jnp.where(visible, jnp.exp(masked - top_value), 0.0)
    prob_step = exp_terms / lax.optimization_barrier(jnp.sum(exp_terms, axis=1, keepdims=True)) - target

    def grad_head(key_grad, head_index):
        query_head, activation, weight_col = index_slices(head_index)
        grad_terms = jnp.where(activation > 0.0, prob_step * weight_col * inv_scale, 0.0).astype(jnp.bfloat16)
        query_grad = jnp.dot(grad_terms, index_keys, preferred_element_type=jnp.float32)
        key_grad = key_grad + jnp.dot(grad_terms.T, query_head, preferred_element_type=jnp.float32)
        return (key_grad, query_grad)
    key_grad, query_stack = lax.scan(grad_head, jnp.zeros((KEYS, IDIM), jnp.float32), jnp.arange(IHEADS, dtype=jnp.int32))
    query_grad = jnp.transpose(query_stack, (1, 0, 2)).reshape(QUERIES, IHEADS * IDIM)
    return (query_grad, key_grad)
```

```python
import functools
import math

import jax
import jax.numpy as jnp
from jax import lax
from jax.experimental import pallas as pl
from jax.experimental.pallas import tpu as pltpu
from jax.sharding import PartitionSpec as P

HEADS = 128
HEAD_DIM = 192
IDIM = 128
STRIDE = 8
NEG_FILL = -1e30
LOG2E = math.log2(math.e)
BLOCKS = 4
MESH = pl.DeviceIdType.MESH
F32 = jnp.float32
BF16 = jnp.bfloat16
NT = (((1,), (1,)), ((), ()))


def matmul_nt(a, b):
    return lax.dot_general(a, b, NT, preferred_element_type=F32)


def kernel(
    n_ctx, n_head, heads,
    q_hbm, k_hbm, iq_hbm, ik_ref, hwt_ref, hwcol_ref, qpos_ref, koff_ref,
    qgrad_ref, kgrad_ref,
    q_v, k_v, iq_v, probs, ikg, bias, lg_part, lg_recv, expo,
    stat_send, stat_recv, ist_send, ist_recv, w_send, w_recv, wi_ref,
    tg_part, tg_recv, pst, ps_send, ps_recv, kg_part, kg_recv, qg, hwb, iqo,
    q_sem, k_sem, iq_sem, ag_s, ag_r, lg_s, lg_r, st_s, st_r, is_s, is_r,
    w_s, w_r, tg_s, tg_r, ps_s, ps_r, kg_s, kg_r,
):
    me = lax.axis_index("ctx")
    my_head = lax.axis_index("head")
    pairs, rows, pair_width = q_v.shape
    keys = k_v.shape[1]
    iheads = iq_v.shape[0]
    own = rows // n_ctx
    per_owner = max(1, 2 * pairs // n_ctx)
    split = n_ctx * per_owner // (2 * pairs)
    part_rows = rows // split
    half = keys // 2
    block = keys // BLOCKS
    score_scale = LOG2E / math.sqrt(HEAD_DIM)
    inv_scale = 1.0 / math.sqrt(IDIM)

    def peer_of(k, n, base):
        return lax.rem(base + k, n)

    def q_copy(p):
        cols = pl.ds(pl.multiple_of(p * pair_width, 128), pair_width)
        return pltpu.make_async_copy(q_hbm.at[:, cols], q_v.at[p], q_sem.at[p])

    def k_copy(p):
        cols = pl.ds(pl.multiple_of(p * pair_width, 128), pair_width)
        return pltpu.make_async_copy(k_hbm.at[:, cols], k_v.at[p], k_sem.at[p])

    def iq_copy(j):
        cols = pl.ds(pl.multiple_of(j * IDIM, 128), IDIM)
        return pltpu.make_async_copy(iq_hbm.at[:, cols], iq_v.at[j], iq_sem.at[j])

    @pl.loop(0, iheads)
    def _(j):
        iq_copy(j).start()

    @pl.loop(0, pairs)
    def _(p):
        q_copy(p).start()
        k_copy(p).start()

    barrier = pltpu.get_barrier_semaphore()
    for k in range(1, n_ctx):
        pl.semaphore_signal(
            barrier, inc=1, device_id={"ctx": peer_of(k, n_ctx, me)}, device_id_type=MESH
        )
    for k in range(1, n_head):
        pl.semaphore_signal(
            barrier, inc=1, device_id={"head": peer_of(k, n_head, my_head)}, device_id_type=MESH
        )

    ikg[me] = ik_ref[...].astype(F32)
    key_pos = STRIDE * (me * keys + lax.broadcasted_iota(jnp.int32, (keys, 1), 0)) + koff_ref[...]
    bias[...] = jnp.where(key_pos <= qpos_ref[...], 0.0, NEG_FILL)
    hwb[...] = jnp.broadcast_to(hwcol_ref[...] * inv_scale, hwb.shape)
    lg_part[...] = jnp.zeros_like(lg_part)

    pl.semaphore_wait(barrier, n_ctx - 1 + n_head - 1)

    bits = [1 << b for b in reversed(range(n_ctx.bit_length() - 1))]

    def flip(index, bit):
        return index + bit * (1 - 2 * lax.rem(lax.div(index, bit), 2))

    def ag_shards(stage, base):
        shards = [base]
        for bit in bits[:stage]:
            shards = shards + [flip(s, bit) for s in shards]
        return shards

    def ag_copy(shard, stage):
        return pltpu.make_async_remote_copy(
            src_ref=ikg.at[shard], dst_ref=ikg.at[shard],
            send_sem=ag_s.at[stage, shard], recv_sem=ag_r.at[shard],
            device_id={"ctx": flip(me, bits[stage])}, device_id_type=MESH,
        )

    def ag_start(stage):
        for shard in ag_shards(stage, me):
            ag_copy(shard, stage).start()

    def ag_recv(stage):
        for shard in ag_shards(stage, flip(me, bits[stage])):
            ag_copy(shard, stage).wait_recv()

    def ag_sent(stage):
        for shard in ag_shards(stage, me):
            ag_copy(shard, stage).wait_send()

    stages = len(bits)
    ag_start(0)

    @pl.loop(0, iheads)
    def _(j):
        iq_copy(j).wait()
        act = matmul_nt(ik_ref[...], iq_v[j])
        weight = hwt_ref[pl.ds(j, 1), :] * inv_scale
        lg_part[...] += weight * jnp.maximum(act, 0.0)

    def head_copy(k, src, dst, send, recv):
        return pltpu.make_async_remote_copy(
            src_ref=src, dst_ref=dst, send_sem=send, recv_sem=recv,
            device_id={"head": peer_of(k, n_head, my_head)}, device_id_type=MESH,
        )

    def lg_copy(k, slot):
        return head_copy(k, lg_part, lg_recv.at[slot], lg_s.at[k], lg_r.at[slot])

    for k in range(1, n_head):
        lg_copy(k, my_head).start()

    column = lax.broadcasted_iota(jnp.int32, (keys, 256), 1)

    def attn_pair(p):
        q_copy(p).wait()
        k_copy(p).wait()
        for a in range(2):
            kept = column < HEAD_DIM if a == 0 else column >= 256 - HEAD_DIM
            k_head = k_v[p, :, a * 128 : a * 128 + 256]
            k_head = jnp.where(kept, k_head, jnp.zeros_like(k_head))
            scores = matmul_nt(k_head, q_v[p, :, a * 128 : a * 128 + 256])
            scores = scores * score_scale + bias[...]
            top = jnp.max(scores, axis=0, keepdims=True)
            expo_head = jnp.exp2(scores - top)
            mass = jnp.sum(expo_head, axis=0, keepdims=True)
            head = 2 * p + a
            probs[head] = expo_head.astype(BF16)
            owner = lax.div(head, per_owner) * split
            row = lax.rem(head, per_owner)
            for part in range(split):
                lanes = slice(part * part_rows, (part + 1) * part_rows)
                stat_send[owner + part, pl.ds(row, 1), :] = top[:, lanes]
                stat_send[owner + part, pl.ds(row + per_owner, 1), :] = mass[:, lanes]

    cuts = [pairs * s // (stages - 1) for s in range(stages)]
    for s in range(stages - 1):
        pl.loop(cuts[s], cuts[s + 1])(attn_pair)
        ag_recv(s)
        ag_start(s + 1)

    for k in range(1, n_head):
        slot = peer_of(k, n_head, my_head)
        lg_copy(k, slot).wait_recv()
    logits = lg_part[...]
    for k in range(1, n_head):
        logits = logits + lg_recv[peer_of(k, n_head, my_head)]
    logits = logits * LOG2E + bias[...]
    itop = jnp.max(logits, axis=0, keepdims=True)
    logits = jnp.exp2(logits - itop)
    expo[...] = logits
    ist_send[0:1, :] = itop
    ist_send[1:2, :] = jnp.sum(logits, axis=0, keepdims=True)

    def ctx_copy(k, src, dst, send, recv):
        return pltpu.make_async_remote_copy(
            src_ref=src, dst_ref=dst, send_sem=send, recv_sem=recv,
            device_id={"ctx": peer_of(k, n_ctx, me)}, device_id_type=MESH,
        )

    def stat_copy(k, peer, slot):
        return ctx_copy(k, stat_send.at[peer], stat_recv.at[slot], st_s.at[k], st_r.at[slot])

    def ist_copy(k, slot):
        return ctx_copy(k, ist_send, ist_recv.at[slot], is_s.at[k], is_r.at[slot])

    def w_copy(k, peer, slot):
        return ctx_copy(k, w_send.at[peer], w_recv.at[slot], w_s.at[k], w_r.at[slot])

    def ps_copy(c, k, peer, slot):
        return ctx_copy(
            k, ps_send.at[c, peer], ps_recv.at[c, slot], ps_s.at[c, k], ps_r.at[c, slot]
        )

    @pl.loop(1, n_ctx)
    def _(k):
        peer = peer_of(k, n_ctx, me)
        stat_copy(k, peer, me).start()
        ist_copy(k, me).start()

    stat_recv[me] = stat_send[me]
    ist_recv[me] = ist_send[...]

    @pl.loop(1, n_ctx)
    def _(k):
        peer = peer_of(k, n_ctx, me)
        stat_copy(k, peer, peer).wait_recv()

    tops = stat_recv[:, :per_owner, :]
    masses = stat_recv[:, per_owner:, :]
    top = jnp.max(tops, axis=0, keepdims=True)
    shift = jnp.exp2(tops - top)
    total = jnp.sum(masses * shift, axis=0, keepdims=True)
    w_send[...] = shift * (1.0 / (HEADS * total))

    @pl.loop(1, n_ctx)
    def _(k):
        peer = peer_of(k, n_ctx, me)
        w_copy(k, peer, me).start()

    w_recv[me] = w_send[me]

    @pl.loop(1, n_ctx)
    def _(k):
        peer = peer_of(k, n_ctx, me)
        ist_copy(k, peer).wait_recv()

    itops = ist_recv[:, 0:1, :]
    imasses = ist_recv[:, 1:2, :]
    itop_all = jnp.max(itops, axis=0)
    itotal = jnp.sum(imasses * jnp.exp2(itops - itop_all[None]), axis=0)
    wi_ref[...] = jnp.exp2(ist_send[0:1, :] - itop_all) / itotal

    @pl.loop(1, n_ctx)
    def _(k):
        peer = peer_of(k, n_ctx, me)
        w_copy(k, peer, peer).wait_recv()

    def tg_copy(k, b, slot):
        span = pl.ds(b * block, block)
        return head_copy(
            k, tg_part.at[span], tg_recv.at[slot, span], tg_s.at[b, k], tg_r.at[b, slot]
        )

    for b in range(BLOCKS):
        for c in range(rows // 256):
            lanes = slice(c * 256, (c + 1) * 256)

            part, start = c * 256 // part_rows, c * 256 % part_rows

            def add_owner(o, acc):
                weights = w_recv[o * split + part, :, start : start + 256]
                for r in range(per_owner):
                    terms = probs[o * per_owner + r, b * block : (b + 1) * block, lanes]
                    acc = acc + terms.astype(F32) * weights[r : r + 1]
                return acc

            tg_part[b * block : (b + 1) * block, lanes] = lax.fori_loop(
                0, n_ctx // split, add_owner, jnp.zeros((block, 256), F32)
            )
        for k in range(1, n_head):
            tg_copy(k, b, my_head).start()

    for s in range(stages - 1, stages):
        ag_recv(s)

    for c in range(2):
        for b in range(c * BLOCKS // 2, (c + 1) * BLOCKS // 2):
            for k in range(1, n_head):
                tg_copy(k, b, peer_of(k, n_head, my_head)).wait_recv()
        span = slice(c * half, (c + 1) * half)
        target = tg_part[span]
        for k in range(1, n_head):
            target = target + tg_recv[peer_of(k, n_head, my_head), span]
        step = expo[span] * wi_ref[...] - target
        pst[span] = step
        ps_send[c] = step.T.reshape(n_ctx, own, half)

        @pl.loop(1, n_ctx)
        def _(k):
            peer = peer_of(k, n_ctx, me)
            ps_copy(c, k, peer, me).start()

        ps_recv[c, me] = ps_send[c, me]

    kg_part[...] = jnp.zeros_like(kg_part)

    @pl.loop(0, iheads)
    def _(j):
        act = matmul_nt(ik_ref[...], iq_v[j])
        weight = hwt_ref[pl.ds(j, 1), :] * inv_scale
        terms = jnp.where(act > 0.0, pst[...] * weight, 0.0).astype(BF16)
        kg_part[...] += jnp.dot(terms, iq_v[j], preferred_element_type=F32)

    def kg_copy(k, slot):
        return head_copy(k, kg_part, kg_recv.at[slot], kg_s.at[k], kg_r.at[slot])

    for k in range(1, n_head):
        kg_copy(k, my_head).start()

    first = pl.multiple_of(me * own, own)
    for j in range(iheads):
        iqo[j * own : (j + 1) * own, :] = iq_v[j, pl.ds(first, own), :]
    qg[...] = jnp.zeros_like(qg)

    def add_source(source):
        source_keys = ikg[source].astype(BF16)
        act = matmul_nt(iqo[...], source_keys)
        terms = []
        for c in range(2):
            step = ps_recv[c, source]
            weighted = hwb[...].reshape(iheads, own, half) * step[None]
            positive = act[:, c * half : (c + 1) * half] > 0.0
            terms.append(
                jnp.where(positive, weighted.reshape(iheads * own, half), 0.0).astype(BF16)
            )
        qg[...] += jnp.dot(
            jnp.concatenate(terms, axis=1), source_keys, preferred_element_type=F32
        )

    add_source(me)

    @pl.loop(1, n_ctx)
    def _(k):
        source = peer_of(k, n_ctx, me)
        for c in range(2):
            ps_copy(c, k, source, source).wait_recv()
        add_source(source)

    for j in range(iheads):
        qgrad_ref[:, j * IDIM : (j + 1) * IDIM] = qg[j * own : (j + 1) * own, :]

    key_grad = kg_part[...]
    for k in range(1, n_head):
        slot = peer_of(k, n_head, my_head)
        kg_copy(k, slot).wait_recv()
        key_grad = key_grad + kg_recv[slot]
    kgrad_ref[...] = key_grad

    for s in range(stages):
        ag_sent(s)
    for k in range(1, n_head):
        lg_copy(k, my_head).wait_send()
        kg_copy(k, my_head).wait_send()
        for b in range(BLOCKS):
            tg_copy(k, b, my_head).wait_send()

    @pl.loop(1, n_ctx)
    def _(k):
        peer = peer_of(k, n_ctx, me)
        stat_copy(k, peer, me).wait_send()
        ist_copy(k, me).wait_send()
        w_copy(k, peer, me).wait_send()
        for c in range(2):
            ps_copy(c, k, peer, me).wait_send()


def shards(n_ctx, n_head, queries, attn_keys, index_queries, index_keys, head_weights, query_pos, key_offset):
    rows = queries.shape[0]
    keys = attn_keys.shape[0]
    heads = attn_keys.shape[1] // HEAD_DIM
    iheads = index_queries.shape[1] // IDIM
    own = rows // n_ctx
    pairs = heads // 2
    per_owner = max(1, heads // n_ctx)
    split = n_ctx * per_owner // heads
    stages = n_ctx.bit_length() - 1
    own_weights = lax.dynamic_slice_in_dim(head_weights, lax.axis_index("ctx") * own, own, 0)
    weight_col = own_weights.T.reshape(iheads * own, 1)
    vmem = pltpu.VMEM
    dma = pltpu.SemaphoreType.DMA
    any_space = pl.BlockSpec(memory_space=pl.ANY)
    vmem_space = pl.BlockSpec(memory_space=pltpu.VMEM)
    return pl.pallas_call(
        functools.partial(kernel, n_ctx, n_head, heads),
        out_shape=(
            jax.ShapeDtypeStruct((own, iheads * IDIM), F32),
            jax.ShapeDtypeStruct((keys, IDIM), F32),
        ),
        in_specs=[any_space] * 3 + [vmem_space] * 5,
        out_specs=(vmem_space, vmem_space),
        scratch_shapes=[
            vmem((pairs, rows, 2 * HEAD_DIM), BF16),
            vmem((pairs, keys, 2 * HEAD_DIM), BF16),
            vmem((iheads, rows, IDIM), BF16),
            vmem((heads, keys, rows), BF16),
            vmem((n_ctx, keys, IDIM), F32),
            vmem((keys, rows), F32),
            vmem((keys, rows), F32),
            vmem((n_head, keys, rows), F32),
            vmem((keys, rows), F32),
            vmem((n_ctx, 2 * per_owner, rows // split), F32),
            vmem((n_ctx, 2 * per_owner, rows // split), F32),
            vmem((2, rows), F32),
            vmem((n_ctx, 2, rows), F32),
            vmem((n_ctx, per_owner, rows // split), F32),
            vmem((n_ctx, per_owner, rows // split), F32),
            vmem((1, rows), F32),
            vmem((keys, rows), F32),
            vmem((n_head, keys, rows), F32),
            vmem((keys, rows), F32),
            vmem((2, n_ctx, own, keys // 2), F32),
            vmem((2, n_ctx, own, keys // 2), F32),
            vmem((keys, IDIM), F32),
            vmem((n_head, keys, IDIM), F32),
            vmem((iheads * own, IDIM), F32),
            vmem((iheads * own, keys // 2), F32),
            vmem((iheads * own, IDIM), BF16),
            dma((pairs,)),
            dma((pairs,)),
            dma((iheads,)),
            dma((stages, n_ctx)),
            dma((n_ctx,)),
            dma((n_head,)),
            dma((n_head,)),
            dma((n_ctx,)),
            dma((n_ctx,)),
            dma((n_ctx,)),
            dma((n_ctx,)),
            dma((n_ctx,)),
            dma((n_ctx,)),
            dma((BLOCKS, n_head)),
            dma((BLOCKS, n_head)),
            dma((2, n_ctx)),
            dma((2, n_ctx)),
            dma((n_head,)),
            dma((n_head,)),
        ],
        compiler_params=pltpu.CompilerParams(
            collective_id=0, has_side_effects=True, vmem_limit_bytes=64 * 1024 * 1024 - 65536
        ),
    )(
        queries,
        attn_keys,
        index_queries,
        index_keys,
        head_weights.T,
        weight_col,
        query_pos.reshape(1, rows),
        key_offset.reshape(keys, 1),
    )


def solution(mesh):
    in_specs = (
        P(None, "head"),
        P("ctx", "head"),
        P(None, "head"),
        P("ctx", None),
        P(None, "head"),
        P(),
        P("ctx"),
    )
    out_specs = (P("ctx", "head"), P("ctx", None))
    body = functools.partial(shards, mesh.shape["ctx"], mesh.shape["head"])
    return jax.shard_map(body, mesh=mesh, in_specs=in_specs, out_specs=out_specs, check_vma=False)
```

```python
import functools
import math

import jax
import jax.numpy as jnp
from jax import lax
from jax.experimental import pallas as pl
from jax.experimental.pallas import tpu as pltpu
from jax.sharding import PartitionSpec as P

HEADS = 128
HEAD_DIM = 192
IDIM = 128
STRIDE = 8
NEG_FILL = -1e30
LOG2E = math.log2(math.e)
BLOCKS = 2
MESH = pl.DeviceIdType.MESH
F32 = jnp.float32
BF16 = jnp.bfloat16
NT = (((1,), (1,)), ((), ()))


def matmul_nt(a, b):
    return lax.dot_general(a, b, NT, preferred_element_type=F32)


def kernel(
    n_ctx, n_head, heads,
    q_hbm, k_hbm, iq_hbm, ik_ref, hwt_ref, qpos_ref, koff_ref,
    qgrad_ref, kgrad_ref,
    q_v, k_v, iq_v, probs, ikg, bias, lg_part, lg_recv, expo,
    stat_send, stat_recv, ist_send, ist_recv, w_send, w_recv, wi_ref,
    tg_part, tg_recv, pst, ps_send, ps_recv, kg_part, kg_recv, qg, hwb, hw_rows, iqo,
    q_sem, k_sem, iq_sem, ag_s, ag_r, lg_s, lg_r, st_s, st_r, is_s, is_r,
    w_s, w_r, tg_s, tg_r, ps_s, ps_r, kg_s, kg_r,
):
    me = lax.axis_index("ctx")
    my_head = lax.axis_index("head")
    pairs, rows, pair_width = q_v.shape
    keys = k_v.shape[1]
    iheads = iq_v.shape[0]
    own = rows // n_ctx
    per_owner = max(1, 2 * pairs // n_ctx)
    split = n_ctx * per_owner // (2 * pairs)
    lanes_half = rows // 2
    part_rows = lanes_half // split
    block = keys // BLOCKS
    score_scale = LOG2E / math.sqrt(HEAD_DIM)
    inv_scale = 1.0 / math.sqrt(IDIM)

    def peer_of(k, n, base):
        return lax.rem(base + k, n)

    def q_copy(p):
        cols = pl.ds(pl.multiple_of(p * pair_width, 128), pair_width)
        return pltpu.make_async_copy(q_hbm.at[:, cols], q_v.at[p], q_sem.at[p])

    def k_copy(p):
        cols = pl.ds(pl.multiple_of(p * pair_width, 128), pair_width)
        return pltpu.make_async_copy(k_hbm.at[:, cols], k_v.at[p], k_sem.at[p])

    def iq_copy(j):
        cols = pl.ds(pl.multiple_of(j * IDIM, 128), IDIM)
        return pltpu.make_async_copy(iq_hbm.at[:, cols], iq_v.at[j], iq_sem.at[j])

    @pl.loop(0, iheads)
    def _(j):
        iq_copy(j).start()

    @pl.loop(0, pairs)
    def _(p):
        q_copy(p).start()
        k_copy(p).start()

    barrier = pltpu.get_barrier_semaphore()
    for k in range(1, n_ctx):
        pl.semaphore_signal(
            barrier, inc=1, device_id={"ctx": peer_of(k, n_ctx, me)}, device_id_type=MESH
        )
    for k in range(1, n_head):
        pl.semaphore_signal(
            barrier, inc=1, device_id={"head": peer_of(k, n_head, my_head)}, device_id_type=MESH
        )

    ikg[me] = ik_ref[...].astype(F32)
    offset = jnp.broadcast_to(koff_ref[...].astype(F32), (128, keys)).T[:, 0:1].astype(jnp.int32)
    key_pos = STRIDE * (me * keys + lax.broadcasted_iota(jnp.int32, (keys, 1), 0)) + offset
    bias[...] = jnp.where(key_pos <= qpos_ref[...], 0.0, NEG_FILL)
    hw_rows[...] = hwt_ref[...].T * inv_scale
    own_weights = hw_rows[pl.ds(pl.multiple_of(me * own, own), own), :]
    for j in range(iheads):
        hwb[j * own : (j + 1) * own, :] = jnp.broadcast_to(own_weights[:, j : j + 1], (own, 128))
    lg_part[...] = jnp.zeros_like(lg_part)

    pl.semaphore_wait(barrier, n_ctx - 1 + n_head - 1)

    bits = [1 << b for b in reversed(range(n_ctx.bit_length() - 1))]

    def flip(index, bit):
        return index + bit * (1 - 2 * lax.rem(lax.div(index, bit), 2))

    def ag_shards(stage, base):
        shards = [base]
        for bit in bits[:stage]:
            shards = shards + [flip(s, bit) for s in shards]
        return shards

    sub_rows = keys // 2

    def ag_copy(shard, sub, stage):
        piece = ikg.at[shard, pl.ds(sub * sub_rows, sub_rows)]
        return pltpu.make_async_remote_copy(
            src_ref=piece, dst_ref=piece,
            send_sem=ag_s.at[stage, sub, shard], recv_sem=ag_r.at[sub, shard],
            device_id={"ctx": flip(me, bits[stage])}, device_id_type=MESH,
        )

    def ag_start(sub, stage):
        for shard in ag_shards(stage, me):
            ag_copy(shard, sub, stage).start()

    def ag_recv(sub, stage):
        for shard in ag_shards(stage, flip(me, bits[stage])):
            ag_copy(shard, sub, stage).wait_recv()

    def ag_sent(sub, stage):
        for shard in ag_shards(stage, me):
            ag_copy(shard, sub, stage).wait_send()

    def ag_forward(event):
        sub, stage = event % 2, event // 2
        ag_recv(sub, stage)
        ag_start(sub, stage + 1)

    stages = len(bits)
    forwards = 2 * (stages - 1)
    for sub in range(2):
        ag_start(sub, 0)

    @pl.loop(0, iheads)
    def _(j):
        iq_copy(j).wait()
        act = matmul_nt(ik_ref[...], iq_v[j])
        weight = hwt_ref[pl.ds(j, 1), :] * inv_scale
        lg_part[...] += weight * jnp.maximum(act, 0.0)

    def head_copy(k, src, dst, send, recv):
        return pltpu.make_async_remote_copy(
            src_ref=src, dst_ref=dst, send_sem=send, recv_sem=recv,
            device_id={"head": peer_of(k, n_head, my_head)}, device_id_type=MESH,
        )

    def lg_copy(k, slot):
        return head_copy(k, lg_part, lg_recv.at[slot], lg_s.at[k], lg_r.at[slot])

    for k in range(1, n_head):
        lg_copy(k, my_head).start()

    def ctx_copy(k, src, dst, send, recv):
        return pltpu.make_async_remote_copy(
            src_ref=src, dst_ref=dst, send_sem=send, recv_sem=recv,
            device_id={"ctx": peer_of(k, n_ctx, me)}, device_id_type=MESH,
        )

    def stat_copy(h, k, peer, slot):
        return ctx_copy(
            k, stat_send.at[h, peer], stat_recv.at[h, slot], st_s.at[h, k], st_r.at[h, slot]
        )

    def ist_copy(k, slot):
        return ctx_copy(k, ist_send, ist_recv.at[slot], is_s.at[k], is_r.at[slot])

    def w_copy(h, k, peer, slot):
        return ctx_copy(k, w_send.at[h, peer], w_recv.at[h, slot], w_s.at[h, k], w_r.at[h, slot])

    def ps_copy(peer, slot):
        return pltpu.make_async_remote_copy(
            src_ref=ps_send.at[peer], dst_ref=ps_recv.at[slot],
            send_sem=ps_s.at[peer], recv_sem=ps_r.at[slot],
            device_id={"ctx": peer}, device_id_type=MESH,
        )

    def send_stats(h):
        @pl.loop(1, n_ctx)
        def _(k):
            stat_copy(h, k, peer_of(k, n_ctx, me), me).start()

        stat_recv[h, me] = stat_send[h, me]

    def send_weights(h):
        @pl.loop(1, n_ctx)
        def _(k):
            peer = peer_of(k, n_ctx, me)
            stat_copy(h, k, peer, peer).wait_recv()

        tops = stat_recv[h, :, :per_owner, :]
        masses = stat_recv[h, :, per_owner:, :]
        top = jnp.max(tops, axis=0, keepdims=True)
        shift = jnp.exp2(tops - top)
        total = jnp.sum(masses * shift, axis=0, keepdims=True)
        w_send[h] = shift * (1.0 / (HEADS * total))

        @pl.loop(1, n_ctx)
        def _(k):
            w_copy(h, k, peer_of(k, n_ctx, me), me).start()

        w_recv[h, me] = w_send[h, me]

    def recv_weights(h):
        @pl.loop(1, n_ctx)
        def _(k):
            peer = peer_of(k, n_ctx, me)
            w_copy(h, k, peer, peer).wait_recv()

    column = lax.broadcasted_iota(jnp.int32, (keys, 256), 1)

    def attn_pair(h, p):
        span = slice(h * lanes_half, (h + 1) * lanes_half)
        for a in range(2):
            kept = column < HEAD_DIM if a == 0 else column >= 256 - HEAD_DIM
            k_head = k_v[p, :, a * 128 : a * 128 + 256]
            k_head = jnp.where(kept, k_head, jnp.zeros_like(k_head))
            scores = matmul_nt(k_head, q_v[p, span, a * 128 : a * 128 + 256])
            scores = scores * score_scale + bias[:, span]
            top = jnp.max(scores, axis=0, keepdims=True)
            expo_head = jnp.exp2(scores - top)
            mass = jnp.sum(expo_head, axis=0, keepdims=True)
            head = 2 * p + a
            probs[head, :, span] = expo_head.astype(BF16)
            owner = lax.div(head, per_owner) * split
            row = lax.rem(head, per_owner)
            for part in range(split):
                lanes = slice(part * part_rows, (part + 1) * part_rows)
                stat_send[h, owner + part, pl.ds(row, 1), :] = top[:, lanes]
                stat_send[h, owner + part, pl.ds(row + per_owner, 1), :] = mass[:, lanes]

    ag_forward(0)
    for h in range(2):
        events = {}
        for event in range(1, forwards):
            at = event * 2 * pairs // forwards
            if at // pairs == h:
                events.setdefault(at % pairs, []).append(event)

        @pl.loop(0, pairs)
        def _(p):
            if h == 0:
                q_copy(p).wait()
                k_copy(p).wait()
            attn_pair(h, p)
            if h == 1:
                pl.when(p == pairs // 2)(functools.partial(send_weights, 0))
            for at, forwarded in events.items():

                @pl.when(p == at)
                def _():
                    for event in forwarded:
                        ag_forward(event)

        send_stats(h)

    for k in range(1, n_head):
        slot = peer_of(k, n_head, my_head)
        lg_copy(k, slot).wait_recv()
    logits = lg_part[...]
    for k in range(1, n_head):
        logits = logits + lg_recv[peer_of(k, n_head, my_head)]
    logits = logits * LOG2E + bias[...]
    itop = jnp.max(logits, axis=0, keepdims=True)
    logits = jnp.exp2(logits - itop)
    expo[...] = logits
    ist_send[0:1, :] = itop
    ist_send[1:2, :] = jnp.sum(logits, axis=0, keepdims=True)

    @pl.loop(1, n_ctx)
    def _(k):
        ist_copy(k, me).start()

    ist_recv[me] = ist_send[...]

    def tg_copy(h, b, k, slot):
        span = pl.ds(b * block, block)
        return head_copy(
            k, tg_part.at[h, span], tg_recv.at[slot, h, span],
            tg_s.at[h, b, k], tg_r.at[h, b, slot],
        )

    width = min(256, part_rows)

    def sum_heads(h, b):
        span = slice(b * block, (b + 1) * block)
        for c in range(lanes_half // width):
            part, start = c * width // part_rows, c * width % part_rows
            lanes = slice(h * lanes_half + c * width, h * lanes_half + (c + 1) * width)

            def add_owner(o, acc):
                weights = w_recv[h, o * split + part, :, start : start + width]
                for r in range(per_owner):
                    terms = probs[o * per_owner + r, span, lanes]
                    acc = acc + terms.astype(F32) * weights[r : r + 1]
                return acc

            tg_part[h, span, c * width : (c + 1) * width] = lax.fori_loop(
                0, n_ctx // split, add_owner, jnp.zeros((block, width), F32)
            )
        for k in range(1, n_head):
            tg_copy(h, b, k, my_head).start()

    recv_weights(0)
    for b in range(BLOCKS):
        sum_heads(0, b)
        if b == 0:
            send_weights(1)

    @pl.loop(1, n_ctx)
    def _(k):
        peer = peer_of(k, n_ctx, me)
        ist_copy(k, peer).wait_recv()

    itops = ist_recv[:, 0:1, :]
    imasses = ist_recv[:, 1:2, :]
    itop_all = jnp.max(itops, axis=0)
    itotal = jnp.sum(imasses * jnp.exp2(itops - itop_all[None]), axis=0)
    wi_ref[...] = jnp.exp2(ist_send[0:1, :] - itop_all) / itotal

    recv_weights(1)
    for b in range(BLOCKS):
        sum_heads(1, b)

    owners = n_ctx // 2
    for h in range(2):
        for b in range(BLOCKS):
            for k in range(1, n_head):
                tg_copy(h, b, k, peer_of(k, n_head, my_head)).wait_recv()
        lanes = slice(h * lanes_half, (h + 1) * lanes_half)
        target = tg_part[h]
        for k in range(1, n_head):
            target = target + tg_recv[peer_of(k, n_head, my_head), h]
        step = expo[:, lanes] * wi_ref[:, lanes] - target
        pst[:, lanes] = step
        ps_send[h * owners : (h + 1) * owners] = step.T.reshape(owners, own, keys)

        @pl.loop(0, owners)
        def _(k):
            peer = h * owners + lax.rem(me + k, owners)

            @pl.when(peer != me)
            def _():
                ps_copy(peer, me).start()

    ps_recv[me] = ps_send[me]

    kg_part[...] = jnp.zeros_like(kg_part)

    @pl.loop(0, iheads)
    def _(j):
        act = matmul_nt(ik_ref[...], iq_v[j])
        weight = hwt_ref[pl.ds(j, 1), :] * inv_scale
        terms = jnp.where(act > 0.0, pst[...] * weight, 0.0).astype(BF16)
        kg_part[...] += jnp.dot(terms, iq_v[j], preferred_element_type=F32)

    def kg_copy(k, slot):
        return head_copy(k, kg_part, kg_recv.at[slot], kg_s.at[k], kg_r.at[slot])

    for k in range(1, n_head):
        kg_copy(k, my_head).start()

    first = pl.multiple_of(me * own, own)
    for j in range(iheads):
        iqo[j * own : (j + 1) * own, :] = iq_v[j, pl.ds(first, own), :]
    qg[...] = jnp.zeros_like(qg)

    def add_source(source):
        source_keys = ikg[source].astype(BF16)
        act = matmul_nt(iqo[...], source_keys)
        terms = []
        for c in range(keys // 128):
            lanes = slice(c * 128, (c + 1) * 128)
            step = ps_recv[source, :, lanes]
            weighted = hwb[...].reshape(iheads, own, 128) * step[None]
            terms.append(
                jnp.where(act[:, lanes] > 0.0, weighted.reshape(iheads * own, 128), 0.0).astype(BF16)
            )
        qg[...] += jnp.dot(
            jnp.concatenate(terms, axis=1), source_keys, preferred_element_type=F32
        )

    for sub in range(2):
        ag_recv(sub, stages - 1)

    add_source(me)

    @pl.loop(1, n_ctx)
    def _(k):
        source = peer_of(k, n_ctx, me)
        ps_copy(source, source).wait_recv()
        add_source(source)

    for j in range(iheads):
        qgrad_ref[:, j * IDIM : (j + 1) * IDIM] = qg[j * own : (j + 1) * own, :]

    key_grad = kg_part[...]
    for k in range(1, n_head):
        slot = peer_of(k, n_head, my_head)
        kg_copy(k, slot).wait_recv()
        key_grad = key_grad + kg_recv[slot]
    kgrad_ref[...] = key_grad

    for s in range(stages):
        for sub in range(2):
            ag_sent(sub, s)
    for k in range(1, n_head):
        lg_copy(k, my_head).wait_send()
        kg_copy(k, my_head).wait_send()
        for h in range(2):
            for b in range(BLOCKS):
                tg_copy(h, b, k, my_head).wait_send()

    @pl.loop(1, n_ctx)
    def _(k):
        peer = peer_of(k, n_ctx, me)
        ist_copy(k, me).wait_send()
        for h in range(2):
            stat_copy(h, k, peer, me).wait_send()
            w_copy(h, k, peer, me).wait_send()
        ps_copy(peer, me).wait_send()


def shards(n_ctx, n_head, queries, attn_keys, index_queries, index_keys, head_weights, query_pos, key_offset):
    rows = queries.shape[0]
    keys = attn_keys.shape[0]
    heads = attn_keys.shape[1] // HEAD_DIM
    iheads = index_queries.shape[1] // IDIM
    own = rows // n_ctx
    pairs = heads // 2
    per_owner = max(1, heads // n_ctx)
    split = n_ctx * per_owner // heads
    stages = n_ctx.bit_length() - 1
    vmem = pltpu.VMEM
    dma = pltpu.SemaphoreType.DMA
    any_space = pl.BlockSpec(memory_space=pl.ANY)
    vmem_space = pl.BlockSpec(memory_space=pltpu.VMEM)
    return pl.pallas_call(
        functools.partial(kernel, n_ctx, n_head, heads),
        out_shape=(
            jax.ShapeDtypeStruct((own, iheads * IDIM), F32),
            jax.ShapeDtypeStruct((keys, IDIM), F32),
        ),
        in_specs=[any_space] * 3 + [vmem_space] * 4,
        out_specs=(vmem_space, vmem_space),
        scratch_shapes=[
            vmem((pairs, rows, 2 * HEAD_DIM), BF16),
            vmem((pairs, keys, 2 * HEAD_DIM), BF16),
            vmem((iheads, rows, IDIM), BF16),
            vmem((heads, keys, rows), BF16),
            vmem((n_ctx, keys, IDIM), F32),
            vmem((keys, rows), F32),
            vmem((keys, rows), F32),
            vmem((n_head, keys, rows), F32),
            vmem((keys, rows), F32),
            vmem((2, n_ctx, 2 * per_owner, rows // 2 // split), F32),
            vmem((2, n_ctx, 2 * per_owner, rows // 2 // split), F32),
            vmem((2, rows), F32),
            vmem((n_ctx, 2, rows), F32),
            vmem((2, n_ctx, per_owner, rows // 2 // split), F32),
            vmem((2, n_ctx, per_owner, rows // 2 // split), F32),
            vmem((1, rows), F32),
            vmem((2, keys, rows // 2), F32),
            vmem((n_head, 2, keys, rows // 2), F32),
            vmem((keys, rows), F32),
            vmem((n_ctx, own, keys), F32),
            vmem((n_ctx, own, keys), F32),
            vmem((keys, IDIM), F32),
            vmem((n_head, keys, IDIM), F32),
            vmem((iheads * own, IDIM), F32),
            vmem((iheads * own, 128), F32),
            vmem((rows, iheads), F32),
            vmem((iheads * own, IDIM), BF16),
            dma((pairs,)),
            dma((pairs,)),
            dma((iheads,)),
            dma((stages, 2, n_ctx)),
            dma((2, n_ctx)),
            dma((n_head,)),
            dma((n_head,)),
            dma((2, n_ctx)),
            dma((2, n_ctx)),
            dma((n_ctx,)),
            dma((n_ctx,)),
            dma((2, n_ctx)),
            dma((2, n_ctx)),
            dma((2, BLOCKS, n_head)),
            dma((2, BLOCKS, n_head)),
            dma((n_ctx,)),
            dma((n_ctx,)),
            dma((n_head,)),
            dma((n_head,)),
        ],
        compiler_params=pltpu.CompilerParams(
            collective_id=0, has_side_effects=True, vmem_limit_bytes=64 * 1024 * 1024 - 65536
        ),
    )(
        queries,
        attn_keys,
        index_queries,
        index_keys,
        head_weights.T,
        query_pos.reshape(1, rows),
        key_offset.reshape(1, keys),
    )


def solution(mesh):
    in_specs = (
        P(None, "head"),
        P("ctx", "head"),
        P(None, "head"),
        P("ctx", None),
        P(None, "head"),
        P(),
        P("ctx"),
    )
    out_specs = (P("ctx", "head"), P("ctx", None))
    body = functools.partial(shards, mesh.shape["ctx"], mesh.shape["head"])
    return jax.shard_map(body, mesh=mesh, in_specs=in_specs, out_specs=out_specs, check_vma=False)
```

```python
import functools
import math

import jax
import jax.numpy as jnp
from jax import lax
from jax.experimental import pallas as pl
from jax.experimental.pallas import tpu as pltpu
from jax.sharding import PartitionSpec as P

HEADS = 128
HEAD_DIM = 192
IDIM = 128
STRIDE = 8
NEG_FILL = -1e30
LOG2E = math.log2(math.e)
BLOCKS = 2
GROUP = 4
IQ_PARTS = 4
MESH = pl.DeviceIdType.MESH
F32 = jnp.float32
BF16 = jnp.bfloat16
NT = (((1,), (1,)), ((), ()))


def matmul_nt(a, b):
    return lax.dot_general(a, b, NT, preferred_element_type=F32)


def kernel(
    n_ctx, n_head, heads,
    q_hbm, k_hbm, iq_hbm, ik_ref, hwt_ref, qpos_ref, koff_ref,
    qgrad_ref, kgrad_ref,
    q_v, k_v, iq_v, probs, ikg, bias, lg_part, lg_recv, expo,
    stat_send, stat_recv, ist_send, ist_recv, w_send, w_recv, wi_ref,
    tg_part, tg_recv, pst, ps_send, ps_recv, kg_part, kg_recv, qg, hwb, hw_rows, iqo,
    q_sem, k_sem, iq_sem, ag_s, ag_r, lg_s, lg_r, st_s, st_r, is_s, is_r,
    w_s, w_r, tg_s, tg_r, ps_s, ps_r, kg_s, kg_r,
):
    me = lax.axis_index("ctx")
    my_head = lax.axis_index("head")
    groups, rows, group_width = q_v.shape
    pair_width = 2 * HEAD_DIM
    group = group_width // pair_width
    pairs = groups * group
    keys = k_v.shape[1]
    iheads = iq_v.shape[1] // IDIM
    iq_rows = rows // IQ_PARTS
    own = rows // n_ctx
    per_owner = max(1, 2 * pairs // n_ctx)
    split = n_ctx * per_owner // (2 * pairs)
    lanes_half = rows // 2
    part_rows = lanes_half // split
    block = keys // BLOCKS
    score_scale = LOG2E / math.sqrt(HEAD_DIM)
    inv_scale = 1.0 / math.sqrt(IDIM)

    def peer_of(k, n, base):
        return lax.rem(base + k, n)

    def q_copy(p):
        cols = pl.ds(pl.multiple_of(p * group_width, 128), group_width)
        return pltpu.make_async_copy(q_hbm.at[:, cols], q_v.at[p], q_sem.at[p])

    def k_copy(p):
        cols = pl.ds(pl.multiple_of(p * group_width, 128), group_width)
        return pltpu.make_async_copy(k_hbm.at[:, cols], k_v.at[p], k_sem.at[p])

    def iq_copy(j):
        span = pl.ds(pl.multiple_of(j * iq_rows, iq_rows), iq_rows)
        return pltpu.make_async_copy(iq_hbm.at[span], iq_v.at[span], iq_sem.at[j])

    def iq_head(j):
        return iq_v[:, pl.ds(pl.multiple_of(j * IDIM, 128), IDIM)]

    @pl.loop(0, IQ_PARTS)
    def _(j):
        iq_copy(j).start()

    @pl.loop(0, groups)
    def _(p):
        q_copy(p).start()
        k_copy(p).start()

    barrier = pltpu.get_barrier_semaphore()
    for k in range(1, n_ctx):
        pl.semaphore_signal(
            barrier, inc=1, device_id={"ctx": peer_of(k, n_ctx, me)}, device_id_type=MESH
        )
    for k in range(1, n_head):
        pl.semaphore_signal(
            barrier, inc=1, device_id={"head": peer_of(k, n_head, my_head)}, device_id_type=MESH
        )

    ikg[me] = ik_ref[...].astype(F32)
    offset = jnp.broadcast_to(koff_ref[...].astype(F32), (128, keys)).T[:, 0:1].astype(jnp.int32)
    key_pos = STRIDE * (me * keys + lax.broadcasted_iota(jnp.int32, (keys, 1), 0)) + offset
    bias[...] = jnp.where(key_pos <= qpos_ref[...], 0.0, NEG_FILL)
    hw_rows[...] = hwt_ref[...].T * inv_scale
    own_weights = hw_rows[pl.ds(pl.multiple_of(me * own, own), own), :]
    for j in range(iheads):
        hwb[j * own : (j + 1) * own, :] = jnp.broadcast_to(own_weights[:, j : j + 1], (own, 128))
    lg_part[...] = jnp.zeros_like(lg_part)

    pl.semaphore_wait(barrier, n_ctx - 1 + n_head - 1)

    bits = [1 << b for b in reversed(range(n_ctx.bit_length() - 1))]

    def flip(index, bit):
        return index + bit * (1 - 2 * lax.rem(lax.div(index, bit), 2))

    def ag_shards(stage, base):
        shards = [base]
        for bit in bits[:stage]:
            shards = shards + [flip(s, bit) for s in shards]
        return shards

    sub_rows = keys // 2

    def ag_copy(shard, sub, stage):
        piece = ikg.at[shard, pl.ds(sub * sub_rows, sub_rows)]
        return pltpu.make_async_remote_copy(
            src_ref=piece, dst_ref=piece,
            send_sem=ag_s.at[stage, sub, shard], recv_sem=ag_r.at[sub, shard],
            device_id={"ctx": flip(me, bits[stage])}, device_id_type=MESH,
        )

    def ag_start(sub, stage):
        for shard in ag_shards(stage, me):
            ag_copy(shard, sub, stage).start()

    def ag_recv(sub, stage):
        for shard in ag_shards(stage, flip(me, bits[stage])):
            ag_copy(shard, sub, stage).wait_recv()

    def ag_sent(sub, stage):
        for shard in ag_shards(stage, me):
            ag_copy(shard, sub, stage).wait_send()

    def ag_forward(event):
        sub, stage = event % 2, event // 2
        ag_recv(sub, stage)
        ag_start(sub, stage + 1)

    stages = len(bits)
    forwards = 2 * (stages - 1)
    for sub in range(2):
        ag_start(sub, 0)

    @pl.loop(0, IQ_PARTS)
    def _(j):
        iq_copy(j).wait()

    @pl.loop(0, iheads)
    def _(j):
        act = matmul_nt(ik_ref[...], iq_head(j))
        weight = hwt_ref[pl.ds(j, 1), :] * inv_scale
        lg_part[...] += weight * jnp.maximum(act, 0.0)

    def head_copy(k, src, dst, send, recv):
        return pltpu.make_async_remote_copy(
            src_ref=src, dst_ref=dst, send_sem=send, recv_sem=recv,
            device_id={"head": peer_of(k, n_head, my_head)}, device_id_type=MESH,
        )

    def lg_copy(k, slot):
        return head_copy(k, lg_part, lg_recv.at[slot], lg_s.at[k], lg_r.at[slot])

    for k in range(1, n_head):
        lg_copy(k, my_head).start()

    def ctx_copy(k, src, dst, send, recv):
        return pltpu.make_async_remote_copy(
            src_ref=src, dst_ref=dst, send_sem=send, recv_sem=recv,
            device_id={"ctx": peer_of(k, n_ctx, me)}, device_id_type=MESH,
        )

    def stat_copy(h, k, peer, slot):
        return ctx_copy(
            k, stat_send.at[h, peer], stat_recv.at[h, slot], st_s.at[h, k], st_r.at[h, slot]
        )

    def ist_copy(k, slot):
        return ctx_copy(k, ist_send, ist_recv.at[slot], is_s.at[k], is_r.at[slot])

    def w_copy(h, k, peer, slot):
        return ctx_copy(k, w_send.at[h, peer], w_recv.at[h, slot], w_s.at[h, k], w_r.at[h, slot])

    def ps_copy(peer, slot):
        return pltpu.make_async_remote_copy(
            src_ref=ps_send.at[peer], dst_ref=ps_recv.at[slot],
            send_sem=ps_s.at[peer], recv_sem=ps_r.at[slot],
            device_id={"ctx": peer}, device_id_type=MESH,
        )

    def send_stats(h):
        @pl.loop(1, n_ctx)
        def _(k):
            stat_copy(h, k, peer_of(k, n_ctx, me), me).start()

        stat_recv[h, me] = stat_send[h, me]

    def send_weights(h):
        @pl.loop(1, n_ctx)
        def _(k):
            peer = peer_of(k, n_ctx, me)
            stat_copy(h, k, peer, peer).wait_recv()

        tops = stat_recv[h, :, :per_owner, :]
        masses = stat_recv[h, :, per_owner:, :]
        top = jnp.max(tops, axis=0, keepdims=True)
        shift = jnp.exp2(tops - top)
        total = jnp.sum(masses * shift, axis=0, keepdims=True)
        w_send[h] = shift * (1.0 / (HEADS * total))

        @pl.loop(1, n_ctx)
        def _(k):
            w_copy(h, k, peer_of(k, n_ctx, me), me).start()

        w_recv[h, me] = w_send[h, me]

    def recv_weights(h):
        @pl.loop(1, n_ctx)
        def _(k):
            peer = peer_of(k, n_ctx, me)
            w_copy(h, k, peer, peer).wait_recv()

    column = lax.broadcasted_iota(jnp.int32, (keys, 256), 1)

    def attn_pair(h, p):
        span = slice(h * lanes_half, (h + 1) * lanes_half)
        for a in range(2):
            kept = column < HEAD_DIM if a == 0 else column >= 256 - HEAD_DIM
            start = pl.multiple_of(lax.rem(p, group) * pair_width + a * 128, 128)
            k_head = k_v[lax.div(p, group), :, pl.ds(start, 256)]
            k_head = jnp.where(kept, k_head, jnp.zeros_like(k_head))
            scores = matmul_nt(k_head, q_v[lax.div(p, group), span, pl.ds(start, 256)])
            scores = scores * score_scale + bias[:, span]
            top = jnp.max(scores, axis=0, keepdims=True)
            expo_head = jnp.exp2(scores - top)
            mass = jnp.sum(expo_head, axis=0, keepdims=True)
            head = 2 * p + a
            probs[head, :, span] = expo_head.astype(BF16)
            owner = lax.div(head, per_owner) * split
            row = lax.rem(head, per_owner)
            for part in range(split):
                lanes = slice(part * part_rows, (part + 1) * part_rows)
                stat_send[h, owner + part, pl.ds(row, 1), :] = top[:, lanes]
                stat_send[h, owner + part, pl.ds(row + per_owner, 1), :] = mass[:, lanes]

    ag_forward(0)
    for h in range(2):
        events = {}
        for event in range(1, forwards):
            at = event * 2 * pairs // forwards
            if at // pairs == h:
                events.setdefault(at % pairs, []).append(event)

        @pl.loop(0, pairs)
        def _(p):
            if h == 0:

                @pl.when(lax.rem(p, group) == 0)
                def _():
                    q_copy(lax.div(p, group)).wait()
                    k_copy(lax.div(p, group)).wait()

            attn_pair(h, p)
            if h == 1:
                pl.when(p == pairs // 2)(functools.partial(send_weights, 0))
            for at, forwarded in events.items():

                @pl.when(p == at)
                def _():
                    for event in forwarded:
                        ag_forward(event)

        send_stats(h)

    for k in range(1, n_head):
        slot = peer_of(k, n_head, my_head)
        lg_copy(k, slot).wait_recv()
    logits = lg_part[...]
    for k in range(1, n_head):
        logits = logits + lg_recv[peer_of(k, n_head, my_head)]
    logits = logits * LOG2E + bias[...]
    itop = jnp.max(logits, axis=0, keepdims=True)
    logits = jnp.exp2(logits - itop)
    expo[...] = logits
    ist_send[0:1, :] = itop
    ist_send[1:2, :] = jnp.sum(logits, axis=0, keepdims=True)

    @pl.loop(1, n_ctx)
    def _(k):
        ist_copy(k, me).start()

    ist_recv[me] = ist_send[...]

    def tg_copy(h, b, k, slot):
        span = pl.ds(b * block, block)
        return head_copy(
            k, tg_part.at[h, span], tg_recv.at[slot, h, span],
            tg_s.at[h, b, k], tg_r.at[h, b, slot],
        )

    width = min(256, part_rows)

    def sum_heads(h, b):
        span = slice(b * block, (b + 1) * block)
        for c in range(lanes_half // width):
            part, start = c * width // part_rows, c * width % part_rows
            lanes = slice(h * lanes_half + c * width, h * lanes_half + (c + 1) * width)

            def add_owner(o, acc):
                weights = w_recv[h, o * split + part, :, start : start + width]
                for r in range(per_owner):
                    terms = probs[o * per_owner + r, span, lanes]
                    acc = acc + terms.astype(F32) * weights[r : r + 1]
                return acc

            tg_part[h, span, c * width : (c + 1) * width] = lax.fori_loop(
                0, n_ctx // split, add_owner, jnp.zeros((block, width), F32)
            )
        for k in range(1, n_head):
            tg_copy(h, b, k, my_head).start()

    recv_weights(0)
    for b in range(BLOCKS):
        sum_heads(0, b)
        if b == 0:
            send_weights(1)

    @pl.loop(1, n_ctx)
    def _(k):
        peer = peer_of(k, n_ctx, me)
        ist_copy(k, peer).wait_recv()

    itops = ist_recv[:, 0:1, :]
    imasses = ist_recv[:, 1:2, :]
    itop_all = jnp.max(itops, axis=0)
    itotal = jnp.sum(imasses * jnp.exp2(itops - itop_all[None]), axis=0)
    wi_ref[...] = jnp.exp2(ist_send[0:1, :] - itop_all) / itotal

    recv_weights(1)
    for b in range(BLOCKS):
        sum_heads(1, b)

    owners = n_ctx // 2
    for h in range(2):
        for b in range(BLOCKS):
            for k in range(1, n_head):
                tg_copy(h, b, k, peer_of(k, n_head, my_head)).wait_recv()
        lanes = slice(h * lanes_half, (h + 1) * lanes_half)
        target = tg_part[h]
        for k in range(1, n_head):
            target = target + tg_recv[peer_of(k, n_head, my_head), h]
        step = expo[:, lanes] * wi_ref[:, lanes] - target
        pst[:, lanes] = step
        ps_send[h * owners : (h + 1) * owners] = step.T.reshape(owners, own, keys)

        @pl.loop(0, owners)
        def _(k):
            peer = h * owners + lax.rem(me + k, owners)

            @pl.when(peer != me)
            def _():
                ps_copy(peer, me).start()

    ps_recv[me] = ps_send[me]

    kg_part[...] = jnp.zeros_like(kg_part)

    @pl.loop(0, iheads)
    def _(j):
        act = matmul_nt(ik_ref[...], iq_head(j))
        weight = hwt_ref[pl.ds(j, 1), :] * inv_scale
        terms = jnp.where(act > 0.0, pst[...] * weight, 0.0).astype(BF16)
        kg_part[...] += jnp.dot(terms, iq_head(j), preferred_element_type=F32)

    def kg_copy(k, slot):
        return head_copy(k, kg_part, kg_recv.at[slot], kg_s.at[k], kg_r.at[slot])

    for k in range(1, n_head):
        kg_copy(k, my_head).start()

    first = pl.multiple_of(me * own, own)
    for j in range(iheads):
        iqo[j * own : (j + 1) * own, :] = iq_v[pl.ds(first, own), j * IDIM : (j + 1) * IDIM]
    qg[...] = jnp.zeros_like(qg)

    def add_source(source):
        source_keys = ikg[source].astype(BF16)
        act = matmul_nt(iqo[...], source_keys)
        terms = []
        for c in range(keys // 128):
            lanes = slice(c * 128, (c + 1) * 128)
            step = ps_recv[source, :, lanes]
            weighted = hwb[...].reshape(iheads, own, 128) * step[None]
            terms.append(
                jnp.where(act[:, lanes] > 0.0, weighted.reshape(iheads * own, 128), 0.0).astype(BF16)
            )
        qg[...] += jnp.dot(
            jnp.concatenate(terms, axis=1), source_keys, preferred_element_type=F32
        )

    for sub in range(2):
        ag_recv(sub, stages - 1)

    add_source(me)

    @pl.loop(1, n_ctx)
    def _(k):
        source = peer_of(k, n_ctx, me)
        ps_copy(source, source).wait_recv()
        add_source(source)

    for j in range(iheads):
        qgrad_ref[:, j * IDIM : (j + 1) * IDIM] = qg[j * own : (j + 1) * own, :]

    key_grad = kg_part[...]
    for k in range(1, n_head):
        slot = peer_of(k, n_head, my_head)
        kg_copy(k, slot).wait_recv()
        key_grad = key_grad + kg_recv[slot]
    kgrad_ref[...] = key_grad

    for s in range(stages):
        for sub in range(2):
            ag_sent(sub, s)
    for k in range(1, n_head):
        lg_copy(k, my_head).wait_send()
        kg_copy(k, my_head).wait_send()
        for h in range(2):
            for b in range(BLOCKS):
                tg_copy(h, b, k, my_head).wait_send()

    @pl.loop(1, n_ctx)
    def _(k):
        peer = peer_of(k, n_ctx, me)
        ist_copy(k, me).wait_send()
        for h in range(2):
            stat_copy(h, k, peer, me).wait_send()
            w_copy(h, k, peer, me).wait_send()
        ps_copy(peer, me).wait_send()


def shards(n_ctx, n_head, queries, attn_keys, index_queries, index_keys, head_weights, query_pos, key_offset):
    rows = queries.shape[0]
    keys = attn_keys.shape[0]
    heads = attn_keys.shape[1] // HEAD_DIM
    iheads = index_queries.shape[1] // IDIM
    own = rows // n_ctx
    group = math.gcd(GROUP, heads // 2)
    groups = heads // 2 // group
    per_owner = max(1, heads // n_ctx)
    split = n_ctx * per_owner // heads
    stages = n_ctx.bit_length() - 1
    vmem = pltpu.VMEM
    dma = pltpu.SemaphoreType.DMA
    any_space = pl.BlockSpec(memory_space=pl.ANY)
    vmem_space = pl.BlockSpec(memory_space=pltpu.VMEM)
    return pl.pallas_call(
        functools.partial(kernel, n_ctx, n_head, heads),
        out_shape=(
            jax.ShapeDtypeStruct((own, iheads * IDIM), F32),
            jax.ShapeDtypeStruct((keys, IDIM), F32),
        ),
        in_specs=[any_space] * 3 + [vmem_space] * 4,
        out_specs=(vmem_space, vmem_space),
        scratch_shapes=[
            vmem((groups, rows, 2 * HEAD_DIM * group), BF16),
            vmem((groups, keys, 2 * HEAD_DIM * group), BF16),
            vmem((rows, iheads * IDIM), BF16),
            vmem((heads, keys, rows), BF16),
            vmem((n_ctx, keys, IDIM), F32),
            vmem((keys, rows), F32),
            vmem((keys, rows), F32),
            vmem((n_head, keys, rows), F32),
            vmem((keys, rows), F32),
            vmem((2, n_ctx, 2 * per_owner, rows // 2 // split), F32),
            vmem((2, n_ctx, 2 * per_owner, rows // 2 // split), F32),
            vmem((2, rows), F32),
            vmem((n_ctx, 2, rows), F32),
            vmem((2, n_ctx, per_owner, rows // 2 // split), F32),
            vmem((2, n_ctx, per_owner, rows // 2 // split), F32),
            vmem((1, rows), F32),
            vmem((2, keys, rows // 2), F32),
            vmem((n_head, 2, keys, rows // 2), F32),
            vmem((keys, rows), F32),
            vmem((n_ctx, own, keys), F32),
            vmem((n_ctx, own, keys), F32),
            vmem((keys, IDIM), F32),
            vmem((n_head, keys, IDIM), F32),
            vmem((iheads * own, IDIM), F32),
            vmem((iheads * own, 128), F32),
            vmem((rows, iheads), F32),
            vmem((iheads * own, IDIM), BF16),
            dma((groups,)),
            dma((groups,)),
            dma((IQ_PARTS,)),
            dma((stages, 2, n_ctx)),
            dma((2, n_ctx)),
            dma((n_head,)),
            dma((n_head,)),
            dma((2, n_ctx)),
            dma((2, n_ctx)),
            dma((n_ctx,)),
            dma((n_ctx,)),
            dma((2, n_ctx)),
            dma((2, n_ctx)),
            dma((2, BLOCKS, n_head)),
            dma((2, BLOCKS, n_head)),
            dma((n_ctx,)),
            dma((n_ctx,)),
            dma((n_head,)),
            dma((n_head,)),
        ],
        compiler_params=pltpu.CompilerParams(
            collective_id=0, has_side_effects=True, vmem_limit_bytes=64 * 1024 * 1024 - 65536
        ),
    )(
        queries,
        attn_keys,
        index_queries,
        index_keys,
        head_weights.T,
        query_pos.reshape(1, rows),
        key_offset.reshape(1, keys),
    )


def solution(mesh):
    in_specs = (
        P(None, "head"),
        P("ctx", "head"),
        P(None, "head"),
        P("ctx", None),
        P(None, "head"),
        P(),
        P("ctx"),
    )
    out_specs = (P("ctx", "head"), P("ctx", None))
    body = functools.partial(shards, mesh.shape["ctx"], mesh.shape["head"])
    return jax.shard_map(body, mesh=mesh, in_specs=in_specs, out_specs=out_specs, check_vma=False)
```

```python
import functools
import math

import jax
import jax.numpy as jnp
from jax import lax
from jax.experimental import pallas as pl
from jax.experimental.pallas import tpu as pltpu
from jax.sharding import PartitionSpec as P

HEADS = 128
HEAD_DIM = 192
IDIM = 128
STRIDE = 8
NEG_FILL = -1e30
LOG2E = math.log2(math.e)
BLOCKS = 2
GROUP = 4
IQ_PARTS = 4
MESH = pl.DeviceIdType.MESH
F32 = jnp.float32
BF16 = jnp.bfloat16
NT = (((1,), (1,)), ((), ()))


def matmul_nt(a, b):
    return lax.dot_general(a, b, NT, preferred_element_type=F32)


def kernel(
    n_ctx, n_head, heads,
    q_hbm, k_hbm, iq_hbm, ik_ref, hwt_ref, qpos_ref, koff_ref,
    qgrad_ref, kgrad_ref,
    q_v, k_v, iq_v, probs, ikg, bias, lg_part, lg_recv, expo,
    stat_send, stat_recv, ist_send, ist_recv, w_send, w_recv, wi_ref,
    tg_part, tg_recv, pst, ps_send, ps_recv, kg_part, kg_recv, qg, hwb, hw_rows, iqo,
    q_sem, k_sem, iq_sem, ag_s, ag_r, lg_s, lg_r, st_s, st_r, is_s, is_r,
    w_s, w_r, tg_s, tg_r, ps_s, ps_r, kg_s, kg_r,
):
    me = lax.axis_index("ctx")
    my_head = lax.axis_index("head")
    groups, rows, group_width = q_v.shape
    pair_width = 2 * HEAD_DIM
    group = group_width // pair_width
    pairs = groups * group
    keys = k_v.shape[1]
    iheads = iq_v.shape[1] // IDIM
    iq_rows = rows // IQ_PARTS
    own = rows // n_ctx
    per_owner = max(1, 2 * pairs // n_ctx)
    split = n_ctx * per_owner // (2 * pairs)
    lanes_half = rows // 2
    part_rows = lanes_half // split
    block = keys // BLOCKS
    score_scale = LOG2E / math.sqrt(HEAD_DIM)
    inv_scale = 1.0 / math.sqrt(IDIM)

    def peer_of(k, n, base):
        return lax.rem(base + k, n)

    def q_copy(p):
        cols = pl.ds(pl.multiple_of(p * group_width, 128), group_width)
        return pltpu.make_async_copy(q_hbm.at[:, cols], q_v.at[p], q_sem.at[p])

    def k_copy(p):
        cols = pl.ds(pl.multiple_of(p * group_width, 128), group_width)
        return pltpu.make_async_copy(k_hbm.at[:, cols], k_v.at[p], k_sem.at[p])

    def iq_copy(j):
        span = pl.ds(pl.multiple_of(j * iq_rows, iq_rows), iq_rows)
        return pltpu.make_async_copy(iq_hbm.at[span], iq_v.at[span], iq_sem.at[j])

    def iq_head(j):
        return iq_v[:, pl.ds(pl.multiple_of(j * IDIM, 128), IDIM)]

    @pl.loop(0, IQ_PARTS)
    def _(j):
        iq_copy(j).start()

    @pl.loop(0, groups)
    def _(p):
        q_copy(p).start()
        k_copy(p).start()

    barrier = pltpu.get_barrier_semaphore()
    for k in range(1, n_ctx):
        pl.semaphore_signal(
            barrier, inc=1, device_id={"ctx": peer_of(k, n_ctx, me)}, device_id_type=MESH
        )
    for k in range(1, n_head):
        pl.semaphore_signal(
            barrier, inc=1, device_id={"head": peer_of(k, n_head, my_head)}, device_id_type=MESH
        )

    ikg[me] = ik_ref[...].astype(F32)
    offset = jnp.broadcast_to(koff_ref[...].astype(F32), (128, keys)).T[:, 0:1].astype(jnp.int32)
    key_pos = STRIDE * (me * keys + lax.broadcasted_iota(jnp.int32, (keys, 1), 0)) + offset
    bias[...] = jnp.where(key_pos <= qpos_ref[...], 0.0, NEG_FILL)
    hw_rows[...] = hwt_ref[...].T * inv_scale
    own_weights = hw_rows[pl.ds(pl.multiple_of(me * own, own), own), :]
    for j in range(iheads):
        hwb[j * own : (j + 1) * own, :] = jnp.broadcast_to(own_weights[:, j : j + 1], (own, 128))
    lg_part[...] = jnp.zeros_like(lg_part)

    pl.semaphore_wait(barrier, n_ctx - 1 + n_head - 1)

    bits = [1 << b for b in reversed(range(n_ctx.bit_length() - 1))]

    def flip(index, bit):
        return index + bit * (1 - 2 * lax.rem(lax.div(index, bit), 2))

    def ag_shards(stage, base):
        shards = [base]
        for bit in bits[:stage]:
            shards = shards + [flip(s, bit) for s in shards]
        return shards

    sub_rows = keys // 2

    def ag_copy(shard, sub, stage):
        piece = ikg.at[shard, pl.ds(sub * sub_rows, sub_rows)]
        return pltpu.make_async_remote_copy(
            src_ref=piece, dst_ref=piece,
            send_sem=ag_s.at[stage, sub, shard], recv_sem=ag_r.at[sub, shard],
            device_id={"ctx": flip(me, bits[stage])}, device_id_type=MESH,
        )

    def ag_start(sub, stage):
        for shard in ag_shards(stage, me):
            ag_copy(shard, sub, stage).start()

    def ag_recv(sub, stage):
        for shard in ag_shards(stage, flip(me, bits[stage])):
            ag_copy(shard, sub, stage).wait_recv()

    def ag_sent(sub, stage):
        for shard in ag_shards(stage, me):
            ag_copy(shard, sub, stage).wait_send()

    def ag_forward(event):
        sub, stage = event % 2, event // 2
        ag_recv(sub, stage)
        ag_start(sub, stage + 1)

    stages = len(bits)
    forwards = 2 * (stages - 1)
    for sub in range(2):
        ag_start(sub, 0)

    @pl.loop(0, IQ_PARTS)
    def _(j):
        iq_copy(j).wait()

    @pl.loop(0, iheads, unroll=2)
    def _(j):
        act = matmul_nt(ik_ref[...], iq_head(j))
        weight = hwt_ref[pl.ds(j, 1), :] * inv_scale
        lg_part[...] += weight * jnp.maximum(act, 0.0)

    def head_copy(k, src, dst, send, recv):
        return pltpu.make_async_remote_copy(
            src_ref=src, dst_ref=dst, send_sem=send, recv_sem=recv,
            device_id={"head": peer_of(k, n_head, my_head)}, device_id_type=MESH,
        )

    def lg_copy(k, slot):
        return head_copy(k, lg_part, lg_recv.at[slot], lg_s.at[k], lg_r.at[slot])

    for k in range(1, n_head):
        lg_copy(k, my_head).start()

    def ctx_copy(k, src, dst, send, recv):
        return pltpu.make_async_remote_copy(
            src_ref=src, dst_ref=dst, send_sem=send, recv_sem=recv,
            device_id={"ctx": peer_of(k, n_ctx, me)}, device_id_type=MESH,
        )

    def stat_copy(h, k, peer, slot):
        return ctx_copy(
            k, stat_send.at[h, peer], stat_recv.at[h, slot], st_s.at[h, k], st_r.at[h, slot]
        )

    def ist_copy(k, slot):
        return ctx_copy(k, ist_send, ist_recv.at[slot], is_s.at[k], is_r.at[slot])

    def w_copy(h, k, peer, slot):
        return ctx_copy(k, w_send.at[h, peer], w_recv.at[h, slot], w_s.at[h, k], w_r.at[h, slot])

    def ps_copy(peer, slot):
        return pltpu.make_async_remote_copy(
            src_ref=ps_send.at[peer], dst_ref=ps_recv.at[slot],
            send_sem=ps_s.at[peer], recv_sem=ps_r.at[slot],
            device_id={"ctx": peer}, device_id_type=MESH,
        )

    def send_stats(h):
        @pl.loop(1, n_ctx)
        def _(k):
            stat_copy(h, k, peer_of(k, n_ctx, me), me).start()

        stat_recv[h, me] = stat_send[h, me]

    def send_weights(h):
        @pl.loop(1, n_ctx)
        def _(k):
            peer = peer_of(k, n_ctx, me)
            stat_copy(h, k, peer, peer).wait_recv()

        tops = stat_recv[h, :, :per_owner, :]
        masses = stat_recv[h, :, per_owner:, :]
        top = jnp.max(tops, axis=0, keepdims=True)
        shift = jnp.exp2(tops - top)
        total = jnp.sum(masses * shift, axis=0, keepdims=True)
        w_send[h] = shift * (1.0 / (HEADS * total))

        @pl.loop(1, n_ctx)
        def _(k):
            w_copy(h, k, peer_of(k, n_ctx, me), me).start()

        w_recv[h, me] = w_send[h, me]

    def recv_weights(h):
        @pl.loop(1, n_ctx)
        def _(k):
            peer = peer_of(k, n_ctx, me)
            w_copy(h, k, peer, peer).wait_recv()

    column = lax.broadcasted_iota(jnp.int32, (keys, 256), 1)

    def attn_pair(h, p):
        span = slice(h * lanes_half, (h + 1) * lanes_half)
        for a in range(2):
            kept = column < HEAD_DIM if a == 0 else column >= 256 - HEAD_DIM
            start = pl.multiple_of(lax.rem(p, group) * pair_width + a * 128, 128)
            k_head = k_v[lax.div(p, group), :, pl.ds(start, 256)]
            k_head = jnp.where(kept, k_head, jnp.zeros_like(k_head))
            scores = matmul_nt(k_head, q_v[lax.div(p, group), span, pl.ds(start, 256)])
            scores = scores * score_scale + bias[:, span]
            top = jnp.max(scores, axis=0, keepdims=True)
            expo_head = jnp.exp2(scores - top)
            mass = jnp.sum(expo_head, axis=0, keepdims=True)
            head = 2 * p + a
            probs[head, :, span] = expo_head.astype(BF16)
            owner = lax.div(head, per_owner) * split
            row = lax.rem(head, per_owner)
            for part in range(split):
                lanes = slice(part * part_rows, (part + 1) * part_rows)
                stat_send[h, owner + part, pl.ds(row, 1), :] = top[:, lanes]
                stat_send[h, owner + part, pl.ds(row + per_owner, 1), :] = mass[:, lanes]

    ag_forward(0)
    for h in range(2):
        events = {}
        for event in range(1, forwards):
            at = event * 2 * pairs // forwards
            if at // pairs == h:
                events.setdefault(at % pairs, []).append(event)

        @pl.loop(0, pairs)
        def _(p):
            if h == 0:

                @pl.when(lax.rem(p, group) == 0)
                def _():
                    q_copy(lax.div(p, group)).wait()
                    k_copy(lax.div(p, group)).wait()

            attn_pair(h, p)
            if h == 1:
                pl.when(p == pairs // 2)(functools.partial(send_weights, 0))
            for at, forwarded in events.items():

                @pl.when(p == at)
                def _():
                    for event in forwarded:
                        ag_forward(event)

        send_stats(h)

    for k in range(1, n_head):
        slot = peer_of(k, n_head, my_head)
        lg_copy(k, slot).wait_recv()
    logits = lg_part[...]
    for k in range(1, n_head):
        logits = logits + lg_recv[peer_of(k, n_head, my_head)]
    logits = logits * LOG2E + bias[...]
    itop = jnp.max(logits, axis=0, keepdims=True)
    logits = jnp.exp2(logits - itop)
    expo[...] = logits
    ist_send[0:1, :] = itop
    ist_send[1:2, :] = jnp.sum(logits, axis=0, keepdims=True)

    @pl.loop(1, n_ctx)
    def _(k):
        ist_copy(k, me).start()

    ist_recv[me] = ist_send[...]

    def tg_copy(h, b, k, slot):
        span = pl.ds(b * block, block)
        return head_copy(
            k, tg_part.at[h, span], tg_recv.at[slot, h, span],
            tg_s.at[h, b, k], tg_r.at[h, b, slot],
        )

    width = min(256, part_rows)

    def sum_heads(h, b):
        span = slice(b * block, (b + 1) * block)
        for c in range(lanes_half // width):
            part, start = c * width // part_rows, c * width % part_rows
            lanes = slice(h * lanes_half + c * width, h * lanes_half + (c + 1) * width)

            def add_owner(o, acc):
                weights = w_recv[h, o * split + part, :, start : start + width]
                for r in range(per_owner):
                    terms = probs[o * per_owner + r, span, lanes]
                    acc = acc + terms.astype(F32) * weights[r : r + 1]
                return acc

            tg_part[h, span, c * width : (c + 1) * width] = lax.fori_loop(
                0, n_ctx // split, add_owner, jnp.zeros((block, width), F32), unroll=2
            )
        for k in range(1, n_head):
            tg_copy(h, b, k, my_head).start()

    recv_weights(0)
    for b in range(BLOCKS):
        sum_heads(0, b)
        if b == 0:
            send_weights(1)

    @pl.loop(1, n_ctx)
    def _(k):
        peer = peer_of(k, n_ctx, me)
        ist_copy(k, peer).wait_recv()

    itops = ist_recv[:, 0:1, :]
    imasses = ist_recv[:, 1:2, :]
    itop_all = jnp.max(itops, axis=0)
    itotal = jnp.sum(imasses * jnp.exp2(itops - itop_all[None]), axis=0)
    wi_ref[...] = jnp.exp2(ist_send[0:1, :] - itop_all) / itotal

    recv_weights(1)
    for b in range(BLOCKS):
        sum_heads(1, b)

    owners = n_ctx // 2
    for h in range(2):
        for b in range(BLOCKS):
            for k in range(1, n_head):
                tg_copy(h, b, k, peer_of(k, n_head, my_head)).wait_recv()
        lanes = slice(h * lanes_half, (h + 1) * lanes_half)
        target = tg_part[h]
        for k in range(1, n_head):
            target = target + tg_recv[peer_of(k, n_head, my_head), h]
        step = expo[:, lanes] * wi_ref[:, lanes] - target
        pst[:, lanes] = step
        ps_send[h * owners : (h + 1) * owners] = step.T.reshape(owners, own, keys)

        @pl.loop(0, owners)
        def _(k):
            peer = h * owners + lax.rem(me + k, owners)

            @pl.when(peer != me)
            def _():
                ps_copy(peer, me).start()

    ps_recv[me] = ps_send[me]

    kg_part[...] = jnp.zeros_like(kg_part)

    @pl.loop(0, iheads, unroll=2)
    def _(j):
        act = matmul_nt(ik_ref[...], iq_head(j))
        weight = hwt_ref[pl.ds(j, 1), :] * inv_scale
        terms = jnp.where(act > 0.0, pst[...] * weight, 0.0).astype(BF16)
        kg_part[...] += jnp.dot(terms, iq_head(j), preferred_element_type=F32)

    def kg_copy(k, slot):
        return head_copy(k, kg_part, kg_recv.at[slot], kg_s.at[k], kg_r.at[slot])

    for k in range(1, n_head):
        kg_copy(k, my_head).start()

    first = pl.multiple_of(me * own, own)
    for j in range(iheads):
        iqo[j * own : (j + 1) * own, :] = iq_v[pl.ds(first, own), j * IDIM : (j + 1) * IDIM]
    qg[...] = jnp.zeros_like(qg)

    def add_source(source):
        source_keys = ikg[source].astype(BF16)
        act = matmul_nt(iqo[...], source_keys)
        terms = []
        for c in range(keys // 128):
            lanes = slice(c * 128, (c + 1) * 128)
            step = ps_recv[source, :, lanes]
            weighted = hwb[...].reshape(iheads, own, 128) * step[None]
            terms.append(
                jnp.where(act[:, lanes] > 0.0, weighted.reshape(iheads * own, 128), 0.0).astype(BF16)
            )
        qg[...] += jnp.dot(
            jnp.concatenate(terms, axis=1), source_keys, preferred_element_type=F32
        )

    for sub in range(2):
        ag_recv(sub, stages - 1)

    add_source(me)

    @pl.loop(1, n_ctx)
    def _(k):
        source = peer_of(k, n_ctx, me)
        ps_copy(source, source).wait_recv()
        add_source(source)

    for j in range(iheads):
        qgrad_ref[:, j * IDIM : (j + 1) * IDIM] = qg[j * own : (j + 1) * own, :]

    key_grad = kg_part[...]
    for k in range(1, n_head):
        slot = peer_of(k, n_head, my_head)
        kg_copy(k, slot).wait_recv()
        key_grad = key_grad + kg_recv[slot]
    kgrad_ref[...] = key_grad

    for s in range(stages):
        for sub in range(2):
            ag_sent(sub, s)
    for k in range(1, n_head):
        lg_copy(k, my_head).wait_send()
        kg_copy(k, my_head).wait_send()
        for h in range(2):
            for b in range(BLOCKS):
                tg_copy(h, b, k, my_head).wait_send()

    @pl.loop(1, n_ctx)
    def _(k):
        peer = peer_of(k, n_ctx, me)
        ist_copy(k, me).wait_send()
        for h in range(2):
            stat_copy(h, k, peer, me).wait_send()
            w_copy(h, k, peer, me).wait_send()
        ps_copy(peer, me).wait_send()


def shards(n_ctx, n_head, queries, attn_keys, index_queries, index_keys, head_weights, query_pos, key_offset):
    rows = queries.shape[0]
    keys = attn_keys.shape[0]
    heads = attn_keys.shape[1] // HEAD_DIM
    iheads = index_queries.shape[1] // IDIM
    own = rows // n_ctx
    group = math.gcd(GROUP, heads // 2)
    groups = heads // 2 // group
    per_owner = max(1, heads // n_ctx)
    split = n_ctx * per_owner // heads
    stages = n_ctx.bit_length() - 1
    vmem = pltpu.VMEM
    dma = pltpu.SemaphoreType.DMA
    any_space = pl.BlockSpec(memory_space=pl.ANY)
    vmem_space = pl.BlockSpec(memory_space=pltpu.VMEM)
    return pl.pallas_call(
        functools.partial(kernel, n_ctx, n_head, heads),
        out_shape=(
            jax.ShapeDtypeStruct((own, iheads * IDIM), F32),
            jax.ShapeDtypeStruct((keys, IDIM), F32),
        ),
        in_specs=[any_space] * 3 + [vmem_space] * 4,
        out_specs=(vmem_space, vmem_space),
        scratch_shapes=[
            vmem((groups, rows, 2 * HEAD_DIM * group), BF16),
            vmem((groups, keys, 2 * HEAD_DIM * group), BF16),
            vmem((rows, iheads * IDIM), BF16),
            vmem((heads, keys, rows), BF16),
            vmem((n_ctx, keys, IDIM), F32),
            vmem((keys, rows), F32),
            vmem((keys, rows), F32),
            vmem((n_head, keys, rows), F32),
            vmem((keys, rows), F32),
            vmem((2, n_ctx, 2 * per_owner, rows // 2 // split), F32),
            vmem((2, n_ctx, 2 * per_owner, rows // 2 // split), F32),
            vmem((2, rows), F32),
            vmem((n_ctx, 2, rows), F32),
            vmem((2, n_ctx, per_owner, rows // 2 // split), F32),
            vmem((2, n_ctx, per_owner, rows // 2 // split), F32),
            vmem((1, rows), F32),
            vmem((2, keys, rows // 2), F32),
            vmem((n_head, 2, keys, rows // 2), F32),
            vmem((keys, rows), F32),
            vmem((n_ctx, own, keys), F32),
            vmem((n_ctx, own, keys), F32),
            vmem((keys, IDIM), F32),
            vmem((n_head, keys, IDIM), F32),
            vmem((iheads * own, IDIM), F32),
            vmem((iheads * own, 128), F32),
            vmem((rows, iheads), F32),
            vmem((iheads * own, IDIM), BF16),
            dma((groups,)),
            dma((groups,)),
            dma((IQ_PARTS,)),
            dma((stages, 2, n_ctx)),
            dma((2, n_ctx)),
            dma((n_head,)),
            dma((n_head,)),
            dma((2, n_ctx)),
            dma((2, n_ctx)),
            dma((n_ctx,)),
            dma((n_ctx,)),
            dma((2, n_ctx)),
            dma((2, n_ctx)),
            dma((2, BLOCKS, n_head)),
            dma((2, BLOCKS, n_head)),
            dma((n_ctx,)),
            dma((n_ctx,)),
            dma((n_head,)),
            dma((n_head,)),
        ],
        compiler_params=pltpu.CompilerParams(
            collective_id=0, has_side_effects=True, vmem_limit_bytes=64 * 1024 * 1024 - 65536
        ),
    )(
        queries,
        attn_keys,
        index_queries,
        index_keys,
        head_weights.T,
        query_pos.reshape(1, rows),
        key_offset.reshape(1, keys),
    )


def solution(mesh):
    in_specs = (
        P(None, "head"),
        P("ctx", "head"),
        P(None, "head"),
        P("ctx", None),
        P(None, "head"),
        P(),
        P("ctx"),
    )
    out_specs = (P("ctx", "head"), P("ctx", None))
    body = functools.partial(shards, mesh.shape["ctx"], mesh.shape["head"])
    return jax.shard_map(body, mesh=mesh, in_specs=in_specs, out_specs=out_specs, check_vma=False)
```
